32 devices in a mesh: row: 8 (over z, core), feat: 4 (over y, x).
Axes of the slice: x: 2, y: 2, z: 4, core: 2. Of those that a mesh axis runs over, the one named last changes fastest.
Arguments:
- grads: bfloat16 [64, 16384], P(None, ('row', 'feat')), may hold values from -0.75 to 0.75
- codes: int32 [256, 16384], P('feat', 'row'), may hold values from 0 to 127
- node_ids: int32 [16384], P('row'), may hold values from 0 to 7, as said below
- node_slot: int32 [8], replicated, may hold values from 0 to 7, each once
Outputs:
- owned_hist: float32 [8, 64, 32768], P('row', None, 'feat')
The draws below stay inside these ranges and needn't reach their ends.
Inputs may be any that keep to these rules, and one draw needn't show every extreme that they name: `node_ids`: within each panel of 2048 rows the node ids never fall, every node has at most 512 rows in a panel, and every panel has a node with exactly 512 rows.
All inputs are finite; a program needn't handle non-finite values.
Results may differ from the reference program's by a relative error of at most 0.0028.
Values may be sent and summed in bfloat16 or wider, within the bound.
A program may use at most 64 MiB of HBM per device.

```python
import jax
import jax.numpy as jnp
from jax import lax

OUTPUTS = 64
BINS = 128
FEATURES = 256
PANEL = 2048
PANELS = 8
ROWS = 16384
NODES = 8
CAPACITY = 512


def panel_counts(key):

    def counts_of(subkey):
        first_key, second_key = jax.random.split(subkey)
        chosen = jax.random.randint(first_key, (), 0, NODES)
        weights = jax.random.randint(second_key, (NODES,), 2, 4)
        positions = jnp.arange(NODES, dtype=jnp.int32)
        weights = jnp.where(positions == chosen, 0, weights)
        remaining = PANEL - CAPACITY
        shares = weights * remaining // jnp.sum(weights)
        leftover = remaining - jnp.sum(shares)
        ranking = positions - (positions > chosen).astype(jnp.int32)
        extra = jnp.where((positions != chosen) & (ranking < leftover), 1, 0)
        shares = shares + extra
        return jnp.where(positions == chosen, CAPACITY, shares).astype(jnp.int32)
    subkeys = jax.random.split(jax.random.fold_in(key, 7), PANELS)
    return jax.vmap(counts_of)(subkeys)


def draw_node_ids(key, part):
    counts = panel_counts(key)
    ends = jnp.cumsum(counts, axis=1)
    positions = jnp.arange(PANEL, dtype=jnp.int32)
    below = (positions[None, :, None] >= ends[:, None, :]).astype(jnp.int32)
    return jnp.sum(below, axis=2).astype(jnp.int32).reshape(ROWS)


def plant(values, rng, smallest, top_value):
    longest = values.shape.index(max(values.shape))
    spots = []
    for shift in (0, 1):
        where = [jax.random.randint(jax.random.fold_in(rng, axis), (), 0, length) for axis, length in enumerate(values.shape)]
        where[longest] = (where[longest] + shift) % values.shape[longest]
        spots.append(tuple(where))
    return values.at[spots[0]].set(smallest).at[spots[1]].set(top_value)


def level_of(rng, dims, cuts, low, high):
    gain = 1.0
    for position, parts in cuts:
        draws = jax.random.uniform(jax.random.fold_in(jax.random.fold_in(rng, 6), position), (parts,), jnp.float32, low / len(cuts), high / len(cuts))
        gain = gain * jnp.repeat(jnp.exp(draws), dims[position] // parts).reshape((-1,) + (1,) * (len(dims) - 1 - position))
    return gain


def centred(rng, shape, width, bound, shards=(), kind=jnp.bfloat16):
    values = jax.random.normal(rng, shape, jnp.float32) * width
    if len(shards) > 0:
        values = level_of(rng, shape, shards, -0.22, 0.18) * values
    return jnp.clip(values, min=-bound, max=bound).astype(kind)


def setup_inputs(seed: int = 0) -> dict:
    streams_of = jax.random.split(jax.random.key(seed), 5)
    return {
        "grads": centred(streams_of[0], (OUTPUTS, ROWS), 0.125, 0.75, ((1, 32),)),
        "codes": plant(jax.random.randint(streams_of[1], (FEATURES, ROWS), 0, BINS), jax.random.fold_in(streams_of[1], 1), 0, BINS - 1).astype(jnp.int32),
        "node_ids": draw_node_ids(jax.random.fold_in(streams_of[4], 71), 0),
        "node_slot": jax.random.permutation(streams_of[3], NODES).astype(jnp.int32),
    }


def reference(grads, codes, node_ids, node_slot):
    panels = PANELS
    length = grads.shape[1] // panels
    by_panel = grads.reshape(OUTPUTS, panels, length).transpose(1, 2, 0)
    panel_codes = codes.reshape(FEATURES, panels, length).transpose(1, 0, 2)
    panel_ids = node_ids.reshape(panels, length)

    def add_panel(totals, pieces):
        grad_rows, code_rows, id_rows = pieces
        values = grad_rows.astype(jnp.float32)

        def one_feature(feature_codes):
            segment = id_rows * BINS + feature_codes
            return jax.ops.segment_sum(values, segment, num_segments=NODES * BINS)

        partial_sums = lax.map(one_feature, code_rows)
        rounded = lax.optimization_barrier(partial_sums.astype(jnp.bfloat16))
        return totals + rounded.astype(jnp.float32), None

    start_value = jnp.zeros((FEATURES, NODES * BINS, OUTPUTS), jnp.float32)
    totals = lax.scan(add_panel, start_value, (by_panel, panel_codes, panel_ids))[0]
    histogram = totals.reshape(FEATURES, NODES, BINS, OUTPUTS).transpose(1, 3, 0, 2)
    histogram = histogram.reshape(NODES, OUTPUTS, FEATURES * BINS)
    return histogram[node_slot]
```

```python
import functools

import jax
import jax.numpy as jnp
from jax import lax
from jax.experimental import pallas as pl
from jax.experimental.pallas import tpu as pltpu
from jax.sharding import PartitionSpec as P

BINS = 128
LANES = 128
OUTSIDE = 255
UNIT = 16
GROUP = 8
LOW = 32.0
MESH = pl.DeviceIdType.MESH
F8 = jnp.float8_e4m3fn


def loop(start, stop, body):
    lax.fori_loop(start, stop, lambda i, _: (body(i), 0)[1], 0)


def kernel(
    slots, ids_ref, codes_hbm, grads_hbm, out_ref,
    codes_ref, panel_ref, lines_ref, codes_sent, codes_in, grads_sent, grads_in, wide_ref, scale_ref,
    codes_sem, own_sem, group_send, group_recv, code_send, code_recv,
    grad_send, grad_recv, spread_send, spread_recv, *, chunks,
):
    owners, units, _, capacity = codes_in.shape
    groups, share, piece = grads_hbm.shape
    length = ids_ref.shape[0] * LANES
    outputs = groups * share
    chips = owners // 2
    part = units // chunks
    span = capacity + LANES
    reach, tiles = span // LANES, length // LANES
    row, feat = lax.axis_index("row"), lax.axis_index("feat")
    chip, core = row // 2, lax.rem(row, 2)

    def others(body):
        loop(1, groups, lambda d: body(lax.rem(feat + d, groups)))

    def ahead(dz, c):
        return lax.rem(chip + dz, chips) * 2 + lax.rem(core + c, 2)

    def behind(dz, c):
        return lax.rem(chip + chips - dz, chips) * 2 + lax.rem(core + c, 2)

    def home(f):
        return panel_ref.at[:, pl.ds(pl.multiple_of(f * piece, LANES), piece)]

    def group_copy(peer, owner):
        return pltpu.make_async_remote_copy(
            grads_hbm.at[peer], home(owner), group_send.at[peer], group_recv.at[owner], (row, peer), MESH
        )

    def code_copy(c, peer, owner):
        at = pl.ds(c * part, part)
        return pltpu.make_async_remote_copy(
            codes_sent.at[peer, at], codes_in.at[owner, at],
            code_send.at[peer, c], code_recv.at[owner, c], (peer, feat), MESH,
        )

    def grad_copy(peer, owner):
        return pltpu.make_async_remote_copy(
            grads_sent.at[peer], grads_in.at[owner, feat],
            grad_send.at[peer], grad_recv.at[owner], (peer, feat), MESH,
        )

    def spread_copy(p, peer, owner):
        return pltpu.make_async_remote_copy(
            grads_in.at[p, owner], grads_in.at[p, owner],
            spread_send.at[p, peer], spread_recv.at[p, owner], (row, peer), MESH,
        )

    barrier = pltpu.get_barrier_semaphore()
    others(lambda f: pl.semaphore_signal(barrier, 1, device_id=(row, f), device_id_type=MESH))
    loop(1, owners, lambda d: pl.semaphore_signal(
        barrier, 1, device_id=(lax.rem(row + d, owners), feat), device_id_type=MESH))
    own_piece = pltpu.make_async_copy(grads_hbm.at[feat], home(feat), own_sem)

    def codes_load(i):
        at = pl.ds(pl.multiple_of(i * LANES, LANES), LANES)
        return pltpu.make_async_copy(codes_hbm.at[:, at], codes_ref.at[i], codes_sem.at[i])

    own_piece.start()
    loop(0, tiles, lambda i: codes_load(i).start())

    def window(t):
        first = jnp.sum((ids_ref[...] < slots[t]).astype(jnp.int32))
        tile = jnp.minimum(first // LANES, tiles - reach)
        shift = lax.rem(span - (first - tile * LANES), span)

        def take(ref):
            return jnp.concatenate([ref[tile + i] for i in range(reach)], axis=1)

        return take, shift, take(ids_ref) == slots[t]

    def pack_codes(t, ref):
        take, shift, inside = window(t)
        block = take(codes_ref)
        block = jnp.where(jnp.broadcast_to(inside, block.shape), block, OUTSIDE)
        block = pltpu.roll(block, shift, 1)[:, :capacity].astype(jnp.float32).astype(jnp.bfloat16)
        for u in range(units):
            ref[t, u] = block[u * UNIT : (u + 1) * UNIT]

    def packed_grads(t):
        take, shift, inside = window(t)
        block = take(lines_ref)
        block = jnp.where(jnp.broadcast_to(inside, block.shape), block, 0.0)
        return pltpu.roll(block, shift, 1)[:, :capacity].astype(jnp.bfloat16)

    def send_codes(t):
        loop(0, chunks, lambda c: code_copy(c, t, row).start())

    loop(0, tiles, lambda i: codes_load(i).wait())
    for c in range(2):
        pack_codes(ahead(1, c), codes_sent)
    pl.semaphore_wait(barrier, owners + groups - 2)
    others(lambda f: group_copy(f, feat).start())
    for c in range(2):
        send_codes(ahead(1, c))
    pack_codes(ahead(0, 1), codes_sent)
    send_codes(ahead(0, 1))
    pack_codes(row, codes_in)

    own_piece.wait()
    others(lambda f: group_copy(feat, f).wait_recv())
    for i in range(tiles):
        lines_ref[i] = panel_ref[:, i * LANES : (i + 1) * LANES].astype(jnp.float32)
    grads_in[row, feat] = packed_grads(row)
    others(lambda f: spread_copy(row, f, feat).start())

    def send_grads(t):
        grads_sent[t] = packed_grads(t)
        grad_copy(t, row).start()

    send_grads(ahead(0, 1))
    loop(2, owners, lambda i: send_grads(ahead(i // 2, lax.rem(i, 2))))

    def later_codes(i):
        t = ahead(i // 2, lax.rem(i, 2))
        pack_codes(t, codes_sent)
        send_codes(t)

    loop(4, owners, later_codes)

    def forward(p):
        grad_copy(row, p).wait_recv()
        others(lambda f: spread_copy(p, f, feat).start())

    def prepare(panels):
        lines = []
        for p in panels:
            others(lambda f: spread_copy(p, feat, f).wait_recv())
            lines.append(jnp.concatenate(
                [grads_in[p, f].astype(jnp.float32) for f in range(groups)], axis=0))
        top = functools.reduce(jnp.maximum, [jnp.max(jnp.abs(v), axis=1, keepdims=True) for v in lines])
        level = jnp.floor(jnp.log2(jnp.maximum(top, 2.0**-110)))
        up, down = jnp.exp2(6.0 - level), jnp.exp2(level - 6.0)
        for h, v in enumerate(lines):
            at = pl.ds(h * capacity, capacity)
            v = v * jnp.broadcast_to(up, v.shape)
            high = v.astype(F8)
            wide_ref[:outputs, at] = high
            wide_ref[outputs:, at] = ((v - high.astype(jnp.float32)) * LOW).astype(F8)
        scale_ref[...] = jnp.broadcast_to(down, scale_ref.shape)

    base = lax.broadcasted_iota(jnp.int32, (32, capacity), 0)

    def table_of(line):
        rows = jnp.broadcast_to(line, (32, capacity)) - base
        rows = rows.astype(jnp.int8)
        one, zero = jnp.ones(rows.shape, F8), jnp.zeros(rows.shape, F8)
        return jnp.concatenate([jnp.where(rows == jnp.int8(b), one, zero) for b in range(0, BINS, 32)], axis=0)

    def multiply(panels, u, add):
        blocks = [codes_in[p, u].astype(jnp.float32).astype(jnp.int32) for p in panels]
        down = scale_ref[:, :1]
        for s in range(UNIT // GROUP):
            table = jnp.concatenate([
                jnp.concatenate([table_of(b[s * GROUP + q : s * GROUP + q + 1]) for q in range(GROUP)], axis=0)
                for b in blocks], axis=1)
            both = lax.dot_general(
                wide_ref[...], table, (((1,), (1,)), ((), ())), preferred_element_type=jnp.float32)
            tile = both[:outputs] + both[outputs:] * (1.0 / LOW)
            tile = tile * jnp.broadcast_to(down, tile.shape)
            at = pl.ds(pl.multiple_of((u * UNIT + s * GROUP) * BINS, GROUP * BINS), GROUP * BINS)
            out_ref[:, at] = out_ref[:, at] + tile if add else tile

    half = (units + 1) // 2
    mine, twin = ahead(0, 0), ahead(0, 1)
    forward(twin)
    prepare((mine, twin))
    loop(0, chunks, lambda c: code_copy(c, row, twin).wait_recv())
    loop(0, half, lambda u: multiply((mine, twin), u, False))
    for c in range(2):
        forward(behind(1, c))
    loop(half, units, lambda u: multiply((mine, twin), u, False))

    def phase(dz):
        panels = [behind(dz, c) for c in range(2)]

        @pl.when(dz + 1 < chips)
        def _():
            for c in range(2):
                forward(behind(dz + 1, c))

        prepare(panels)

        def chunk(c):
            for p in panels:
                code_copy(c, row, p).wait_recv()
            loop(c * part, c * part + part, lambda u: multiply(panels, u, True))

        loop(0, chunks, chunk)

    loop(1, chips, phase)

    others(lambda f: group_copy(f, feat).wait_send())

    def sent(d):
        t = lax.rem(row + d, owners)
        loop(0, chunks, lambda c: code_copy(c, t, row).wait_send())
        grad_copy(t, row).wait_send()

    loop(1, owners, sent)
    loop(0, owners, lambda p: others(lambda f: spread_copy(p, f, feat).wait_send()))


def on_device(grads, codes, node_ids, node_slot):
    owners = node_slot.shape[0]
    groups = lax.axis_size("feat")
    features, length = codes.shape
    outputs, piece = grads.shape
    share = outputs // groups
    capacity = 2 * length // owners
    units = features // UNIT
    chunks = min(units, 2)
    vectors = pl.BlockSpec(memory_space=pltpu.VMEM)
    anywhere = pl.BlockSpec(memory_space=pl.ANY)
    dma = pltpu.SemaphoreType.DMA
    hist = pl.pallas_call(
        functools.partial(kernel, chunks=chunks),
        out_shape=jax.ShapeDtypeStruct((outputs, features * BINS), jnp.float32),
        in_specs=[pl.BlockSpec(memory_space=pltpu.SMEM), vectors, anywhere, anywhere],
        out_specs=vectors,
        scratch_shapes=[
            pltpu.VMEM((length // LANES, features, LANES), jnp.int32),
            pltpu.VMEM((share, length), jnp.bfloat16),
            pltpu.VMEM((length // LANES, share, LANES), jnp.float32),
            pltpu.VMEM((owners, units, UNIT, capacity), jnp.bfloat16),
            pltpu.VMEM((owners, units, UNIT, capacity), jnp.bfloat16),
            pltpu.VMEM((owners, share, capacity), jnp.bfloat16),
            pltpu.VMEM((owners, groups, share, capacity), jnp.bfloat16),
            pltpu.VMEM((2 * outputs, 2 * capacity), F8),
            pltpu.VMEM((outputs, LANES), jnp.float32),
            dma((length // LANES,)),
            dma,
            dma((groups,)),
            dma((groups,)),
            dma((owners, chunks)),
            dma((owners, chunks)),
            dma((owners,)),
            dma((owners,)),
            dma((owners, groups)),
            dma((owners, groups)),
        ],
        compiler_params=pltpu.CompilerParams(
            collective_id=0, has_side_effects=True, vmem_limit_bytes=40 << 20
        ),
        name="exchange_and_multiply",
    )(node_slot, node_ids.reshape(length // LANES, 1, LANES), codes, grads.reshape(groups, share, piece))
    return hist[None]


def solution(mesh):
    in_specs = (P(None, ("row", "feat")), P("feat", "row"), P("row"), P())
    out_specs = P("row", None, "feat")
    return jax.shard_map(
        on_device, mesh=mesh, in_specs=in_specs, out_specs=out_specs, check_vma=False
    )
```

```python
import functools

import jax
import jax.numpy as jnp
from jax import lax
from jax.experimental import pallas as pl
from jax.experimental.pallas import tpu as pltpu
from jax.sharding import PartitionSpec as P

BINS = 128
LANES = 128
OUTSIDE = 255
UNIT = 16
LOW = 32.0
MESH = pl.DeviceIdType.MESH
F8 = jnp.float8_e4m3fn


def loop(start, stop, body):
    lax.fori_loop(start, stop, lambda i, _: (body(i), 0)[1], 0)


def kernel(
    slots_hbm, ids_hbm, codes_hbm, grads_hbm, out_ref,
    slots, places, ids_ref, codes_ref, panel_ref, lines_ref, codes_sent, codes_in, grads_sent, grads_in, wide_ref, scale_ref,
    slots_sem, ids_sem, codes_sem, own_sem, group_send, group_recv, code_send, code_recv,
    grad_send, grad_recv, spread_send, spread_recv, *, chunks,
):
    owners, units, _, capacity = codes_in.shape
    groups, share, piece = grads_hbm.shape
    length = codes_ref.shape[0] * LANES
    outputs = groups * share
    chips = owners // 2
    part = units // chunks
    span = capacity + LANES
    reach, tiles = span // LANES, length // LANES
    row, feat = lax.axis_index("row"), lax.axis_index("feat")
    chip, core = row // 2, lax.rem(row, 2)

    def others(body):
        loop(1, groups, lambda d: body(lax.rem(feat + d, groups)))

    def ahead(dz, c):
        return lax.rem(chip + dz, chips) * 2 + lax.rem(core + c, 2)

    def behind(dz, c):
        return lax.rem(chip + chips - dz, chips) * 2 + lax.rem(core + c, 2)

    def home(f):
        return panel_ref.at[:, pl.ds(pl.multiple_of(f * piece, LANES), piece)]

    def group_copy(peer, owner):
        return pltpu.make_async_remote_copy(
            grads_hbm.at[peer], home(owner), group_send.at[peer], group_recv.at[owner], (row, peer), MESH
        )

    def code_copy(c, peer, owner):
        at = pl.ds(c * part, part)
        return pltpu.make_async_remote_copy(
            codes_sent.at[peer, at], codes_in.at[owner, at],
            code_send.at[peer, c], code_recv.at[owner, c], (peer, feat), MESH,
        )

    def grad_copy(peer, owner):
        return pltpu.make_async_remote_copy(
            grads_sent.at[peer], grads_in.at[owner, feat],
            grad_send.at[peer], grad_recv.at[owner], (peer, feat), MESH,
        )

    def spread_copy(p, peer, owner):
        return pltpu.make_async_remote_copy(
            grads_in.at[p, owner], grads_in.at[p, owner],
            spread_send.at[p, peer], spread_recv.at[p, owner], (row, peer), MESH,
        )

    barrier = pltpu.get_barrier_semaphore()
    others(lambda f: pl.semaphore_signal(barrier, 1, device_id=(row, f), device_id_type=MESH))
    loop(1, owners, lambda d: pl.semaphore_signal(
        barrier, 1, device_id=(lax.rem(row + d, owners), feat), device_id_type=MESH))
    slots_load = pltpu.make_async_copy(slots_hbm, slots, slots_sem)
    ids_load = pltpu.make_async_copy(ids_hbm, ids_ref, ids_sem)
    own_piece = pltpu.make_async_copy(grads_hbm.at[feat], home(feat), own_sem)

    def codes_load(i):
        at = pl.ds(pl.multiple_of(i * LANES, LANES), LANES)
        return pltpu.make_async_copy(codes_hbm.at[:, at], codes_ref.at[i], codes_sem.at[i])

    slots_load.start()
    ids_load.start()
    loop(0, tiles, lambda i: codes_load(i).start())
    own_piece.start()
    pl.semaphore_wait(barrier, owners + groups - 2)
    others(lambda f: group_copy(f, feat).start())

    slots_load.wait()
    ids_load.wait()
    ids = ids_ref[...]
    for t in range(owners):
        first = jnp.sum((ids < slots[t]).astype(jnp.int32))
        tile = jnp.minimum(first // LANES, tiles - reach)
        places[0, t] = tile
        places[1, t] = lax.rem(span - (first - tile * LANES), span)
        places[2, t] = jnp.sum((ids == slots[t]).astype(jnp.int32))

    def window(ref, t, fill):
        block = jnp.concatenate([ref[places[0, t] + i] for i in range(reach)], axis=1)
        block = pltpu.roll(block, places[1, t], 1)[:, :capacity]
        lane = lax.broadcasted_iota(jnp.int32, block.shape, 1)
        return jnp.where(lane < places[2, t], block, fill)

    def pack_codes(t, ref):
        block = window(codes_ref, t, OUTSIDE).astype(jnp.float32).astype(jnp.bfloat16)
        for u in range(units):
            ref[t, u] = block[u * UNIT : (u + 1) * UNIT]

    def packed_grads(t):
        return window(lines_ref, t, 0.0).astype(jnp.bfloat16)

    def send_codes(i):
        t = ahead(i // 2, lax.rem(i, 2))
        pack_codes(t, codes_sent)
        loop(0, chunks, lambda c: code_copy(c, t, row).start())

    def send_grads(i):
        t = ahead(i // 2, lax.rem(i, 2))
        grads_sent[t] = packed_grads(t)
        grad_copy(t, row).start()

    loop(0, tiles, lambda i: codes_load(i).wait())
    loop(2, 4, send_codes)

    own_piece.wait()
    others(lambda f: group_copy(feat, f).wait_recv())
    for i in range(tiles):
        lines_ref[i] = panel_ref[:, i * LANES : (i + 1) * LANES].astype(jnp.float32)
    loop(1, owners, send_grads)
    grads_in[row, feat] = packed_grads(row)
    others(lambda f: spread_copy(row, f, feat).start())

    send_codes(1)
    loop(4, owners, send_codes)
    pack_codes(row, codes_in)

    def forward(p):
        grad_copy(row, p).wait_recv()
        others(lambda f: spread_copy(p, f, feat).start())

    def prepare(panels):
        lines = []
        for p in panels:
            others(lambda f: spread_copy(p, feat, f).wait_recv())
            lines.append(jnp.concatenate(
                [grads_in[p, f].astype(jnp.float32) for f in range(groups)], axis=0))
        top = functools.reduce(jnp.maximum, [jnp.max(jnp.abs(v), axis=1, keepdims=True) for v in lines])
        level = jnp.floor(jnp.log2(jnp.maximum(top, 2.0**-110)))
        up, down = jnp.exp2(6.0 - level), jnp.exp2(level - 6.0)
        for h, v in enumerate(lines):
            at = pl.ds(h * capacity, capacity)
            v = v * jnp.broadcast_to(up, v.shape)
            high = v.astype(F8)
            wide_ref[:outputs, at] = high
            wide_ref[outputs:, at] = ((v - high.astype(jnp.float32)) * LOW).astype(F8)
        scale_ref[...] = jnp.broadcast_to(down, scale_ref.shape)

    base = lax.broadcasted_iota(jnp.int32, (32, capacity), 0)

    def table_of(line):
        rows = jnp.broadcast_to(line, (32, capacity)) - base
        rows = rows.astype(jnp.int8)
        one, zero = jnp.ones(rows.shape, F8), jnp.zeros(rows.shape, F8)
        return [jnp.where(rows == jnp.int8(b), one, zero) for b in range(0, BINS, 32)]

    def multiply(panels, c, add):
        def table(p):
            block = [codes_in[p, c * part + u].astype(jnp.float32).astype(jnp.int32) for u in range(part)]
            return jnp.concatenate(
                [t for b in block for q in range(UNIT) for t in table_of(b[q : q + 1])], axis=0)

        both = lax.dot_general(
            wide_ref[...], jnp.concatenate([table(p) for p in panels], axis=1),
            (((1,), (1,)), ((), ())), preferred_element_type=jnp.float32)
        tile = both[:outputs] + both[outputs:] * (1.0 / LOW)
        tile = tile * jnp.broadcast_to(scale_ref[:, :1], tile.shape)
        size = part * UNIT * BINS
        at = pl.ds(pl.multiple_of(c * size, size), size)
        out_ref[:, at] = out_ref[:, at] + tile if add else tile

    mine, twin = ahead(0, 0), ahead(0, 1)
    forward(twin)
    for c in range(2):
        forward(behind(1, c))
    prepare((mine, twin))

    def first(c):
        code_copy(c, row, twin).wait_recv()
        multiply((mine, twin), c, False)

    loop(0, chunks // 2, first)
    if chips > 2:
        for c in range(2):
            forward(behind(2, c))
    loop(chunks // 2, chunks, first)

    def phase(dz):
        panels = [behind(dz, c) for c in range(2)]

        @pl.when(dz + 2 < chips)
        def _():
            for c in range(2):
                forward(behind(dz + 2, c))

        prepare(panels)

        def chunk(c):
            for p in panels:
                code_copy(c, row, p).wait_recv()
            multiply(panels, c, True)

        loop(0, chunks, chunk)

    loop(1, chips, phase)

    others(lambda f: group_copy(f, feat).wait_send())

    def sent(d):
        t = lax.rem(row + d, owners)
        loop(0, chunks, lambda c: code_copy(c, t, row).wait_send())
        grad_copy(t, row).wait_send()

    loop(1, owners, sent)
    loop(0, owners, lambda p: others(lambda f: spread_copy(p, f, feat).wait_send()))


def on_device(grads, codes, node_ids, node_slot):
    owners = node_slot.shape[0]
    groups = lax.axis_size("feat")
    features, length = codes.shape
    outputs, piece = grads.shape
    share = outputs // groups
    capacity = 2 * length // owners
    units = features // UNIT
    chunks = min(units, 2)
    vectors = pl.BlockSpec(memory_space=pltpu.VMEM)
    far = pl.BlockSpec(memory_space=pltpu.HBM)
    dma = pltpu.SemaphoreType.DMA
    hist = pl.pallas_call(
        functools.partial(kernel, chunks=chunks),
        out_shape=jax.ShapeDtypeStruct((outputs, features * BINS), jnp.float32),
        in_specs=[far] * 4,
        out_specs=vectors,
        scratch_shapes=[
            pltpu.SMEM(node_slot.shape, jnp.int32),
            pltpu.SMEM((3, owners), jnp.int32),
            pltpu.VMEM((length // LANES, LANES), jnp.int32),
            pltpu.VMEM((length // LANES, features, LANES), jnp.int32),
            pltpu.VMEM((share, length), jnp.bfloat16),
            pltpu.VMEM((length // LANES, share, LANES), jnp.float32),
            pltpu.VMEM((owners, units, UNIT, capacity), jnp.bfloat16),
            pltpu.VMEM((owners, units, UNIT, capacity), jnp.bfloat16),
            pltpu.VMEM((owners, share, capacity), jnp.bfloat16),
            pltpu.VMEM((owners, groups, share, capacity), jnp.bfloat16),
            pltpu.VMEM((2 * outputs, 2 * capacity), F8),
            pltpu.VMEM((outputs, LANES), jnp.float32),
            dma,
            dma,
            dma((length // LANES,)),
            dma,
            dma((groups,)),
            dma((groups,)),
            dma((owners, chunks)),
            dma((owners, chunks)),
            dma((owners,)),
            dma((owners,)),
            dma((owners, groups)),
            dma((owners, groups)),
        ],
        compiler_params=pltpu.CompilerParams(
            collective_id=0, has_side_effects=True, vmem_limit_bytes=40 << 20
        ),
        name="exchange_and_multiply",
    )(*[
        pltpu.with_memory_space_constraint(x, pltpu.HBM)
        for x in (
            node_slot, node_ids.reshape(length // LANES, LANES),
            codes, grads.reshape(groups, share, piece),
        )
    ])
    return hist[None]


def solution(mesh):
    in_specs = (P(None, ("row", "feat")), P("feat", "row"), P("row"), P())
    out_specs = P("row", None, "feat")
    return jax.shard_map(
        on_device, mesh=mesh, in_specs=in_specs, out_specs=out_specs, check_vma=False
    )
```

```python
import functools

import jax
import jax.numpy as jnp
from jax import lax
from jax.experimental import pallas as pl
from jax.experimental.pallas import tpu as pltpu
from jax.sharding import PartitionSpec as P

BINS = 128
LANES = 128
OUTSIDE = 255
UNIT = 16
LOW = 32.0
MESH = pl.DeviceIdType.MESH
F8 = jnp.float8_e4m3fn


def loop(start, stop, body):
    lax.fori_loop(start, stop, lambda i, _: (body(i), 0)[1], 0)


def kernel(
    slots_hbm, ids_hbm, codes_hbm, grads_hbm, out_ref,
    slots, places, ids_ref, codes_ref, panel_ref, lines_ref,
    codes_sent, codes_in, grads_sent, grads_in, twin_sent, wide_ref, scale_ref,
    slots_sem, ids_sem, codes_sem, own_sem, twin_send, twin_recv, group_send, group_recv,
    code_send, code_recv, grad_send, grad_recv, spread_send, spread_recv, *, chunks,
):
    owners, units, _, capacity = codes_in.shape
    groups, share, piece = grads_hbm.shape
    tiles = ids_ref.shape[0]
    outputs = groups * share
    chips = owners // 2
    part = units // chunks
    span = capacity + LANES
    reach = span // LANES
    row, feat = lax.axis_index("row"), lax.axis_index("feat")
    chip, core = row // 2, lax.rem(row, 2)
    twin = chip * 2 + 1 - core

    def others(body):
        loop(1, groups, lambda d: body(lax.rem(feat + d, groups)))

    def ahead(dz, c):
        return lax.rem(chip + dz, chips) * 2 + lax.rem(core + c, 2)

    def behind(dz, c):
        return lax.rem(chip + chips - dz, chips) * 2 + lax.rem(core + c, 2)

    def remote(body):
        loop(2, owners, lambda i: body(ahead(i // 2, lax.rem(i, 2))))

    def home(k, f):
        return panel_ref.at[k, :, pl.ds(pl.multiple_of(f * piece, LANES), piece)]

    def group_copy(k, peer, owner):
        return pltpu.make_async_remote_copy(
            grads_hbm.at[k], home(k, owner), group_send.at[k, peer], group_recv.at[k, owner], (row, peer), MESH
        )

    def twin_copy():
        return pltpu.make_async_remote_copy(
            twin_sent, grads_in.at[row], twin_send, twin_recv, (twin, feat), MESH
        )

    def code_copy(c, peer, owner):
        at = pl.ds(c * part, part)
        return pltpu.make_async_remote_copy(
            codes_sent.at[peer, at], codes_in.at[owner, at],
            code_send.at[peer, c], code_recv.at[owner, c], (peer, feat), MESH,
        )

    def grad_copy(peer, owner):
        return pltpu.make_async_remote_copy(
            grads_sent.at[peer], grads_in.at[owner, feat],
            grad_send.at[peer], grad_recv.at[owner], (peer, feat), MESH,
        )

    def spread_copy(p, peer, owner):
        return pltpu.make_async_remote_copy(
            grads_in.at[p, owner], grads_in.at[p, owner],
            spread_send.at[p, peer], spread_recv.at[p, owner], (row, peer), MESH,
        )

    barrier = pltpu.get_barrier_semaphore()
    others(lambda f: pl.semaphore_signal(barrier, 1, device_id=(row, f), device_id_type=MESH))
    loop(1, owners, lambda d: pl.semaphore_signal(
        barrier, 1, device_id=(lax.rem(row + d, owners), feat), device_id_type=MESH))
    slots_load = pltpu.make_async_copy(slots_hbm, slots, slots_sem)
    ids_load = pltpu.make_async_copy(ids_hbm, ids_ref, ids_sem)
    codes_load = pltpu.make_async_copy(codes_hbm, codes_ref, codes_sem)

    def own_piece(k):
        return pltpu.make_async_copy(grads_hbm.at[k], home(k, feat), own_sem.at[k])

    slots_load.start()
    ids_load.start()
    codes_load.start()
    pl.semaphore_wait(barrier, owners + groups - 2)
    others(lambda f: group_copy(f, f, feat).start())
    own_piece(feat).start()
    others(lambda k: own_piece(k).start())

    def gather(d):
        group_copy(feat, lax.rem(feat + d, groups), feat).start()
        others(lambda k: pl.when(k != lax.rem(feat + d, groups))(
            lambda: group_copy(k, lax.rem(feat + d, groups), feat).start()))

    loop(1, groups, gather)

    slots_load.wait()
    ids_load.wait()
    ids = ids_ref[...]
    for t in range(owners):
        first = jnp.sum((ids < slots[t]).astype(jnp.int32))
        tile = jnp.minimum(first // LANES, tiles - reach)
        places[0, t] = tile
        places[1, t] = lax.rem(span - (first - tile * LANES), span)
        places[2, t] = jnp.sum((ids == slots[t]).astype(jnp.int32))

    def window(take, t, fill):
        block = jnp.concatenate([take(places[0, t] + i) for i in range(reach)], axis=1)
        block = pltpu.roll(block, places[1, t], 1)[:, :capacity]
        lane = lax.broadcasted_iota(jnp.int32, block.shape, 1)
        return jnp.where(lane < places[2, t], block, fill)

    def code_tile(i):
        return jnp.concatenate([codes_ref[g, i] for g in range(codes_ref.shape[0])], axis=0)

    def pack_codes(t, ref):
        block = window(code_tile, t, OUTSIDE).astype(jnp.float32).astype(jnp.bfloat16)
        for u in range(units):
            ref[t, u] = block[u * UNIT : (u + 1) * UNIT]

    def packed_grads(k, t):
        return window(lambda i: lines_ref[k, i], t, 0.0).astype(jnp.bfloat16)

    def unfold(k):
        for i in range(tiles):
            lines_ref[k, i] = panel_ref[k, :, i * LANES : (i + 1) * LANES].astype(jnp.float32)

    def release(dz, c):
        for k in range(2):
            code_copy(c, ahead(dz, k), row).start()

    codes_load.wait()
    loop(2, 4, lambda i: pack_codes(ahead(1, i - 2), codes_sent))
    loop(0, chunks, lambda c: release(1, c))

    own_piece(feat).wait()
    others(lambda f: group_copy(feat, feat, f).wait_recv())
    unfold(feat)

    def send_grads(t):
        grads_sent[t] = packed_grads(feat, t)
        grad_copy(t, row).start()

    remote(send_grads)
    pack_codes(twin, codes_sent)
    loop(0, chunks, lambda c: code_copy(c, twin, row).start())
    pack_codes(row, codes_in)
    loop(4, owners, lambda i: pack_codes(ahead(i // 2, lax.rem(i, 2)), codes_sent))

    def rest(k):
        own_piece(k).wait()
        others(lambda f: group_copy(k, feat, f).wait_recv())
        unfold(k)

    others(rest)

    def both_nodes(k):
        twin_sent[k] = packed_grads(k, twin)
        grads_in[row, k] = packed_grads(k, row)

    loop(0, groups, both_nodes)
    twin_copy().start()

    def forward(p):
        grad_copy(row, p).wait_recv()
        others(lambda f: spread_copy(p, f, feat).start())

    def prepare(panels):
        lines = [
            jnp.concatenate([grads_in[p, f].astype(jnp.float32) for f in range(groups)], axis=0)
            for p in panels
        ]
        top = functools.reduce(jnp.maximum, [jnp.max(jnp.abs(v), axis=1, keepdims=True) for v in lines])
        level = jnp.floor(jnp.log2(jnp.maximum(top, 2.0**-110)))
        up, down = jnp.exp2(6.0 - level), jnp.exp2(level - 6.0)
        for h, v in enumerate(lines):
            at = pl.ds(h * capacity, capacity)
            v = v * jnp.broadcast_to(up, v.shape)
            high = v.astype(F8)
            wide_ref[:outputs, at] = high
            wide_ref[outputs:, at] = ((v - high.astype(jnp.float32)) * LOW).astype(F8)
        scale_ref[...] = jnp.broadcast_to(down, scale_ref.shape)

    base = lax.broadcasted_iota(jnp.int32, (32, capacity), 0)

    def table_of(line):
        rows = jnp.broadcast_to(line, (32, capacity)) - base
        rows = rows.astype(jnp.int8)
        one, zero = jnp.ones(rows.shape, F8), jnp.zeros(rows.shape, F8)
        return [jnp.where(rows == jnp.int8(b), one, zero) for b in range(0, BINS, 32)]

    def multiply(panels, c, add):
        def table(p):
            block = [codes_in[p, c * part + u].astype(jnp.float32).astype(jnp.int32) for u in range(part)]
            return jnp.concatenate(
                [t for b in block for q in range(UNIT) for t in table_of(b[q : q + 1])], axis=0)

        both = lax.dot_general(
            wide_ref[...], jnp.concatenate([table(p) for p in panels], axis=1),
            (((1,), (1,)), ((), ())), preferred_element_type=jnp.float32)
        tile = both[:outputs] + both[outputs:] * (1.0 / LOW)
        tile = tile * jnp.broadcast_to(scale_ref[:, :1], tile.shape)
        size = part * UNIT * BINS
        at = pl.ds(pl.multiple_of(c * size, size), size)
        out_ref[:, at] = out_ref[:, at] + tile if add else tile

    if chips > 1:
        for c in range(2):
            forward(behind(1, c))
    twin_copy().wait_recv()
    prepare((row, twin))

    def first(c):
        if chips > 2:
            release(2, c)
        code_copy(c, row, twin).wait_recv()
        multiply((row, twin), c, False)

    loop(0, 1, first)
    if chips > 2:
        for c in range(2):
            forward(behind(2, c))
    loop(1, chunks, first)

    def phase(dz):
        panels = [behind(dz, c) for c in range(2)]

        @pl.when(dz + 2 < chips)
        def _():
            for c in range(2):
                forward(behind(dz + 2, c))

        for p in panels:
            others(lambda f: spread_copy(p, feat, f).wait_recv())
        prepare(panels)

        def chunk(c):
            @pl.when(dz + 2 < chips)
            def _():
                release(dz + 2, c)

            for p in panels:
                code_copy(c, row, p).wait_recv()
            multiply(panels, c, True)

        loop(0, chunks, chunk)

    loop(1, chips, phase)

    loop(0, groups, lambda k: others(lambda f: group_copy(k, f, feat).wait_send()))
    twin_copy().wait_send()
    loop(0, chunks, lambda c: code_copy(c, twin, row).wait_send())

    def sent(t):
        loop(0, chunks, lambda c: code_copy(c, t, row).wait_send())
        grad_copy(t, row).wait_send()
        others(lambda f: spread_copy(t, f, feat).wait_send())

    remote(sent)


def on_device(grads, codes, node_ids, node_slot):
    owners = node_slot.shape[0]
    groups = lax.axis_size("feat")
    features, length = codes.shape
    outputs, piece = grads.shape
    share = outputs // groups
    capacity = 2 * length // owners
    tiles = length // LANES
    units = features // UNIT
    chunks = min(units, 2)
    vectors = pl.BlockSpec(memory_space=pltpu.VMEM)
    far = pl.BlockSpec(memory_space=pltpu.HBM)
    dma = pltpu.SemaphoreType.DMA
    hist = pl.pallas_call(
        functools.partial(kernel, chunks=chunks),
        out_shape=jax.ShapeDtypeStruct((outputs, features * BINS), jnp.float32),
        in_specs=[far] * 4,
        out_specs=vectors,
        scratch_shapes=[
            pltpu.SMEM(node_slot.shape, jnp.int32),
            pltpu.SMEM((3, owners), jnp.int32),
            pltpu.VMEM((tiles, LANES), jnp.int32),
            pltpu.VMEM((features // 8, tiles, 8, LANES), jnp.int32),
            pltpu.VMEM((groups, share, length), jnp.bfloat16),
            pltpu.VMEM((groups, tiles, share, LANES), jnp.float32),
            pltpu.VMEM((owners, units, UNIT, capacity), jnp.bfloat16),
            pltpu.VMEM((owners, units, UNIT, capacity), jnp.bfloat16),
            pltpu.VMEM((owners, share, capacity), jnp.bfloat16),
            pltpu.VMEM((owners, groups, share, capacity), jnp.bfloat16),
            pltpu.VMEM((groups, share, capacity), jnp.bfloat16),
            pltpu.VMEM((2 * outputs, 2 * capacity), F8),
            pltpu.VMEM((outputs, LANES), jnp.float32),
            dma,
            dma,
            dma,
            dma((groups,)),
            dma,
            dma,
            dma((groups, groups)),
            dma((groups, groups)),
            dma((owners, chunks)),
            dma((owners, chunks)),
            dma((owners,)),
            dma((owners,)),
            dma((owners, groups)),
            dma((owners, groups)),
        ],
        compiler_params=pltpu.CompilerParams(
            collective_id=0, has_side_effects=True, vmem_limit_bytes=40 << 20
        ),
        name="exchange_and_multiply",
    )(*[
        pltpu.with_memory_space_constraint(x, pltpu.HBM)
        for x in (
            node_slot, node_ids.reshape(tiles, LANES),
            codes.reshape(features // 8, 8, tiles, LANES).transpose(0, 2, 1, 3),
            grads.reshape(groups, share, piece),
        )
    ])
    return hist[None]


def solution(mesh):
    in_specs = (P(None, ("row", "feat")), P("feat", "row"), P("row"), P())
    out_specs = P("row", None, "feat")
    return jax.shard_map(
        on_device, mesh=mesh, in_specs=in_specs, out_specs=out_specs, check_vma=False
    )
```

```python
import functools

import jax
import jax.numpy as jnp
from jax import lax
from jax.experimental import pallas as pl
from jax.experimental.pallas import tpu as pltpu
from jax.sharding import PartitionSpec as P

BINS = 128
LANES = 128
OUTSIDE = 255
UNIT = 16
LOW = 32.0
MESH = pl.DeviceIdType.MESH
F8 = jnp.float8_e4m3fn


def loop(start, stop, body):
    if stop - start <= 8:
        for i in range(start, stop):
            body(i)
    else:
        lax.fori_loop(start, stop, lambda i, _: (body(i), 0)[1], 0)


def kernel(
    slots_hbm, ids_hbm, codes_hbm, grads_hbm, out_ref,
    slots, places, ids_ref, codes_ref, panel_ref, lines_ref,
    codes_sent, codes_in, grads_sent, grads_in, twin_sent, wide_ref, scale_ref,
    slots_sem, ids_sem, codes_sem, own_sem, twin_send, twin_recv, group_send, group_recv,
    code_send, code_recv, grad_send, grad_recv, spread_send, spread_recv, *, chunks,
):
    owners, units, _, capacity = codes_in.shape
    groups, share, piece = grads_hbm.shape
    tiles = ids_ref.shape[0]
    outputs = groups * share
    chips = owners // 2
    part = units // chunks
    span = capacity + LANES
    reach = span // LANES
    row, feat = lax.axis_index("row"), lax.axis_index("feat")
    chip, core = row // 2, lax.rem(row, 2)
    twin = chip * 2 + 1 - core

    def others(body):
        loop(1, groups, lambda d: body(lax.rem(feat + d, groups)))

    def ahead(dz, c):
        return lax.rem(chip + dz, chips) * 2 + lax.rem(core + c, 2)

    def behind(dz, c):
        return lax.rem(chip + chips - dz, chips) * 2 + lax.rem(core + c, 2)

    def remote(body):
        loop(2, owners, lambda i: body(ahead(i // 2, lax.rem(i, 2))))

    def home(f, pieces=1):
        return panel_ref.at[:, :, pl.ds(pl.multiple_of(f * piece, LANES), pieces * piece)]

    def group_copy(peer):
        return pltpu.make_async_remote_copy(
            grads_hbm, home(feat), group_send, group_recv, (row, peer), MESH
        )

    def twin_copy():
        return pltpu.make_async_remote_copy(
            twin_sent, grads_in.at[row], twin_send, twin_recv, (twin, feat), MESH
        )

    def code_copy(c, peer, owner):
        at = pl.ds(c * part, part)
        return pltpu.make_async_remote_copy(
            codes_sent.at[peer, at], codes_in.at[owner, at],
            code_send, code_recv.at[owner, c], (peer, feat), MESH,
        )

    def grad_copy(peer, owner):
        return pltpu.make_async_remote_copy(
            grads_sent.at[peer], grads_in.at[owner, feat],
            grad_send, grad_recv.at[owner], (peer, feat), MESH,
        )

    def spread_copy(p, peer):
        return pltpu.make_async_remote_copy(
            grads_in.at[p, feat], grads_in.at[p, feat],
            spread_send, spread_recv.at[p], (row, peer), MESH,
        )

    def arrive(ref, sem):
        pltpu.make_async_copy(ref, ref, sem).wait()

    barrier = pltpu.get_barrier_semaphore()
    others(lambda f: pl.semaphore_signal(barrier, 1, device_id=(row, f), device_id_type=MESH))
    loop(1, owners, lambda d: pl.semaphore_signal(
        barrier, 1, device_id=(lax.rem(row + d, owners), feat), device_id_type=MESH))
    slots_load = pltpu.make_async_copy(slots_hbm, slots, slots_sem)
    ids_load = pltpu.make_async_copy(ids_hbm, ids_ref, ids_sem)
    codes_load = pltpu.make_async_copy(codes_hbm, codes_ref, codes_sem)

    own_piece = pltpu.make_async_copy(grads_hbm, home(feat), own_sem)
    slots_load.start()
    ids_load.start()
    codes_load.start()
    pl.semaphore_wait(barrier, owners + groups - 2)
    others(lambda f: group_copy(f).start())
    own_piece.start()

    slots_load.wait()
    ids_load.wait()
    ids = ids_ref[...]
    for t in range(owners):
        first = jnp.sum((ids < slots[t]).astype(jnp.int32))
        tile = jnp.minimum(first // LANES, tiles - reach)
        places[0, t] = tile
        places[1, t] = lax.rem(span - (first - tile * LANES), span)
        places[2, t] = jnp.sum((ids == slots[t]).astype(jnp.int32))

    def window(take, t, fill):
        block = jnp.concatenate([take(places[0, t] + i) for i in range(reach)], axis=1)
        block = pltpu.roll(block, places[1, t], 1)[:, :capacity]
        lane = lax.broadcasted_iota(jnp.int32, block.shape, 1)
        return jnp.where(lane < places[2, t], block, fill)

    def code_tile(i):
        return jnp.concatenate([codes_ref[g, i] for g in range(codes_ref.shape[0])], axis=0)

    def pack_codes(t, ref):
        block = window(code_tile, t, OUTSIDE).astype(jnp.float32).astype(jnp.bfloat16)
        for u in range(units):
            ref[t, u] = block[u * UNIT : (u + 1) * UNIT]

    def packed_grads(k, t):
        return window(lambda i: lines_ref[k, i], t, 0.0).astype(jnp.bfloat16)

    def unfold(k):
        for i in range(tiles):
            lines_ref[k, i] = panel_ref[k, :, i * LANES : (i + 1) * LANES].astype(jnp.float32)

    def release(dz, c):
        for k in range(2):
            code_copy(c, ahead(dz, k), row).start()

    codes_load.wait()
    loop(2, 4, lambda i: pack_codes(ahead(1, i - 2), codes_sent))
    loop(0, chunks, lambda c: release(1, c))

    pack_codes(twin, codes_sent)
    loop(0, chunks, lambda c: code_copy(c, twin, row).start())
    pack_codes(row, codes_in)
    loop(4, owners, lambda i: pack_codes(ahead(i // 2, lax.rem(i, 2)), codes_sent))

    own_piece.wait()
    arrive(home(0, groups - 1), group_recv)
    for k in range(groups):
        unfold(k)
    for k in range(groups):
        twin_sent[k] = packed_grads(k, twin)
    twin_copy().start()
    for k in range(groups):
        grads_in[row, k] = packed_grads(k, row)

    def send_grads(t):
        grads_sent[t] = packed_grads(feat, t)
        grad_copy(t, row).start()

    remote(send_grads)

    def forward(p):
        grad_copy(row, p).wait_recv()
        others(lambda f: spread_copy(p, f).start())

    def prepare(panels):
        lines = [
            jnp.concatenate([grads_in[p, f].astype(jnp.float32) for f in range(groups)], axis=0)
            for p in panels
        ]
        top = functools.reduce(jnp.maximum, [jnp.max(jnp.abs(v), axis=1, keepdims=True) for v in lines])
        level = jnp.floor(jnp.log2(jnp.maximum(top, 2.0**-110)))
        up, down = jnp.exp2(6.0 - level), jnp.exp2(level - 6.0)
        for h, v in enumerate(lines):
            at = pl.ds(h * capacity, capacity)
            v = v * jnp.broadcast_to(up, v.shape)
            high = v.astype(F8)
            wide_ref[:outputs, at] = high
            wide_ref[outputs:, at] = ((v - high.astype(jnp.float32)) * LOW).astype(F8)
        scale_ref[...] = jnp.broadcast_to(down, scale_ref.shape)

    base = lax.broadcasted_iota(jnp.int32, (32, capacity), 0)

    def table_of(line):
        rows = jnp.broadcast_to(line, (32, capacity)) - base
        rows = rows.astype(jnp.int8)
        one, zero = jnp.ones(rows.shape, F8), jnp.zeros(rows.shape, F8)
        return [jnp.where(rows == jnp.int8(b), one, zero) for b in range(0, BINS, 32)]

    def multiply(panels, c, add):
        def table(p):
            block = [codes_in[p, c * part + u].astype(jnp.float32).astype(jnp.int32) for u in range(part)]
            return jnp.concatenate(
                [t for b in block for q in range(UNIT) for t in table_of(b[q : q + 1])], axis=0)

        both = lax.dot_general(
            wide_ref[...], jnp.concatenate([table(p) for p in panels], axis=1),
            (((1,), (1,)), ((), ())), preferred_element_type=jnp.float32)
        tile = both[:outputs] + both[outputs:] * (1.0 / LOW)
        tile = tile * jnp.broadcast_to(scale_ref[:, :1], tile.shape)
        size = part * UNIT * BINS
        at = pl.ds(pl.multiple_of(c * size, size), size)
        out_ref[:, at] = out_ref[:, at] + tile if add else tile

    if chips > 1:
        for c in range(2):
            forward(behind(1, c))
    twin_copy().wait_recv()
    prepare((row, twin))

    def first(c):
        if chips > 2:
            release(2, c)
        code_copy(c, row, twin).wait_recv()
        multiply((row, twin), c, False)

    loop(0, 1, first)
    if chips > 2:
        for c in range(2):
            forward(behind(2, c))
    loop(1, chunks, first)

    def phase(dz):
        panels = [behind(dz, c) for c in range(2)]

        @pl.when(jnp.int32(dz + 2) < chips)
        def _():
            for c in range(2):
                forward(behind(dz + 2, c))

        for p in panels:
            arrive(grads_in.at[p, pl.ds(0, groups - 1)], spread_recv.at[p])
        prepare(panels)

        def chunk(c):
            @pl.when(jnp.int32(dz + 2) < chips)
            def _():
                release(dz + 2, c)

            for p in panels:
                code_copy(c, row, p).wait_recv()
            multiply(panels, c, True)

        lax.fori_loop(0, chunks, lambda i, _: (chunk(i), 0)[1], 0)

    lax.fori_loop(1, chips, lambda i, _: (phase(i), 0)[1], 0)

    arrive(home(0, groups - 1), group_send)
    twin_copy().wait_send()
    arrive(codes_sent.at[pl.ds(0, owners - 1)], code_send)
    arrive(grads_sent.at[pl.ds(0, owners - 2)], grad_send)
    arrive(grads_in.at[pl.ds(0, owners - 2), pl.ds(0, groups - 1)], spread_send)


def on_device(grads, codes, node_ids, node_slot):
    owners = node_slot.shape[0]
    groups = lax.axis_size("feat")
    features, length = codes.shape
    outputs, piece = grads.shape
    share = outputs // groups
    capacity = 2 * length // owners
    tiles = length // LANES
    units = features // UNIT
    chunks = min(units, 2)
    vectors = pl.BlockSpec(memory_space=pltpu.VMEM)
    far = pl.BlockSpec(memory_space=pltpu.HBM)
    dma = pltpu.SemaphoreType.DMA
    hist = pl.pallas_call(
        functools.partial(kernel, chunks=chunks),
        out_shape=jax.ShapeDtypeStruct((outputs, features * BINS), jnp.float32),
        in_specs=[far] * 4,
        out_specs=vectors,
        scratch_shapes=[
            pltpu.SMEM(node_slot.shape, jnp.int32),
            pltpu.SMEM((3, owners), jnp.int32),
            pltpu.VMEM((tiles, LANES), jnp.int32),
            pltpu.VMEM((features // 8, tiles, 8, LANES), jnp.int32),
            pltpu.VMEM((groups, share, length), jnp.bfloat16),
            pltpu.VMEM((groups, tiles, share, LANES), jnp.float32),
            pltpu.VMEM((owners, units, UNIT, capacity), jnp.bfloat16),
            pltpu.VMEM((owners, units, UNIT, capacity), jnp.bfloat16),
            pltpu.VMEM((owners, share, capacity), jnp.bfloat16),
            pltpu.VMEM((owners, groups, share, capacity), jnp.bfloat16),
            pltpu.VMEM((groups, share, capacity), jnp.bfloat16),
            pltpu.VMEM((2 * outputs, 2 * capacity), F8),
            pltpu.VMEM((outputs, LANES), jnp.float32),
            dma,
            dma,
            dma,
            dma,
            dma,
            dma,
            dma,
            dma,
            dma,
            dma((owners, chunks)),
            dma,
            dma((owners,)),
            dma,
            dma((owners,)),
        ],
        compiler_params=pltpu.CompilerParams(
            collective_id=0, has_side_effects=True, vmem_limit_bytes=40 << 20
        ),
        name="exchange_and_multiply",
    )(*[
        pltpu.with_memory_space_constraint(x, pltpu.HBM)
        for x in (
            node_slot, node_ids.reshape(tiles, LANES),
            codes.reshape(features // 8, 8, tiles, LANES).transpose(0, 2, 1, 3),
            grads.reshape(groups, share, piece),
        )
    ])
    return hist[None]


def solution(mesh):
    in_specs = (P(None, ("row", "feat")), P("feat", "row"), P("row"), P())
    out_specs = P("row", None, "feat")
    return jax.shard_map(
        on_device, mesh=mesh, in_specs=in_specs, out_specs=out_specs, check_vma=False
    )
```

```python
import functools

import jax
import jax.numpy as jnp
from jax import lax
from jax.experimental import pallas as pl
from jax.experimental.pallas import tpu as pltpu
from jax.sharding import PartitionSpec as P

BINS = 128
LANES = 128
OUTSIDE = 255
UNIT = 16
LOW = 32.0
MESH = pl.DeviceIdType.MESH
F8 = jnp.float8_e4m3fn


def loop(start, stop, body):
    if stop - start <= 8:
        for i in range(start, stop):
            body(i)
    else:
        lax.fori_loop(start, stop, lambda i, _: (body(i), 0)[1], 0)


def table_of(line):
    shape = (32, line.shape[1])
    rows = (jnp.broadcast_to(line, shape) - lax.broadcasted_iota(jnp.int32, shape, 0)).astype(jnp.int8)
    one, zero = jnp.ones(shape, F8), jnp.zeros(shape, F8)
    return [jnp.where(rows == jnp.int8(b), one, zero) for b in range(0, BINS, 32)]


def product(wide, scale, blocks):
    def table(units):
        block = [u.astype(jnp.float32).astype(jnp.int32) for u in units]
        return jnp.concatenate([t for b in block for q in range(UNIT) for t in table_of(b[q : q + 1])], axis=0)

    both = lax.dot_general(
        wide, jnp.concatenate([table(units) for units in blocks], axis=1),
        (((1,), (1,)), ((), ())), preferred_element_type=jnp.float32)
    outputs = both.shape[0] // 2
    tile = both[:outputs] + both[outputs:] * (1.0 / LOW)
    return tile * jnp.broadcast_to(scale, tile.shape)


def kernel(
    slots_hbm, ids_hbm, codes_hbm, grads_hbm, out_ref, last_codes, wide_ref, scale_ref,
    slots, places, ids_ref, codes_ref, panel_ref, lines_ref,
    codes_sent, codes_in, grads_sent, grads_in, twin_sent,
    slots_sem, ids_sem, codes_sem, own_sem, twin_send, twin_recv, group_send, group_recv,
    code_send, code_recv, grad_send, grad_recv, spread_send, spread_recv, *, chunks,
):
    owners, units, _, capacity = codes_in.shape
    groups, share, piece = grads_hbm.shape
    tiles = ids_ref.shape[0]
    outputs = groups * share
    chips = owners // 2
    part = units // chunks
    span = capacity + LANES
    reach = span // LANES
    row, feat = lax.axis_index("row"), lax.axis_index("feat")
    chip, core = row // 2, lax.rem(row, 2)
    twin = chip * 2 + 1 - core

    def others(body):
        loop(1, groups, lambda d: body(lax.rem(feat + d, groups)))

    def ahead(dz, c):
        return lax.rem(chip + dz, chips) * 2 + lax.rem(core + c, 2)

    def behind(dz, c):
        return lax.rem(chip + chips - dz, chips) * 2 + lax.rem(core + c, 2)

    def remote(body):
        loop(2, owners, lambda i: body(ahead(i // 2, lax.rem(i, 2))))

    def home(f, pieces=1):
        return panel_ref.at[:, :, pl.ds(pl.multiple_of(f * piece, LANES), pieces * piece)]

    def group_copy(peer):
        return pltpu.make_async_remote_copy(
            grads_hbm, home(feat), group_send, group_recv, (row, peer), MESH
        )

    def twin_copy():
        return pltpu.make_async_remote_copy(
            twin_sent, grads_in.at[row], twin_send, twin_recv, (twin, feat), MESH
        )

    def code_copy(c, peer, owner):
        at = pl.ds(c * part, part)
        return pltpu.make_async_remote_copy(
            codes_sent.at[peer, at], codes_in.at[owner, at],
            code_send, code_recv.at[owner, c], (peer, feat), MESH,
        )

    def grad_copy(peer, owner):
        return pltpu.make_async_remote_copy(
            grads_sent.at[peer], grads_in.at[owner, feat],
            grad_send, grad_recv.at[owner], (peer, feat), MESH,
        )

    def spread_copy(p, peer):
        return pltpu.make_async_remote_copy(
            grads_in.at[p, feat], grads_in.at[p, feat],
            spread_send, spread_recv.at[p], (row, peer), MESH,
        )

    def arrive(ref, sem):
        pltpu.make_async_copy(ref, ref, sem).wait()

    barrier = pltpu.get_barrier_semaphore()
    others(lambda f: pl.semaphore_signal(barrier, 1, device_id=(row, f), device_id_type=MESH))
    loop(1, owners, lambda d: pl.semaphore_signal(
        barrier, 1, device_id=(lax.rem(row + d, owners), feat), device_id_type=MESH))
    slots_load = pltpu.make_async_copy(slots_hbm, slots, slots_sem)
    ids_load = pltpu.make_async_copy(ids_hbm, ids_ref, ids_sem)
    codes_load = pltpu.make_async_copy(codes_hbm, codes_ref, codes_sem)

    own_piece = pltpu.make_async_copy(grads_hbm, home(feat), own_sem)
    slots_load.start()
    ids_load.start()
    codes_load.start()
    pl.semaphore_wait(barrier, owners + groups - 2)
    others(lambda f: group_copy(f).start())
    own_piece.start()

    slots_load.wait()
    ids_load.wait()
    ids = ids_ref[...]
    for t in range(owners):
        first = jnp.sum((ids < slots[t]).astype(jnp.int32))
        tile = jnp.minimum(first // LANES, tiles - reach)
        places[0, t] = tile
        places[1, t] = lax.rem(span - (first - tile * LANES), span)
        places[2, t] = jnp.sum((ids == slots[t]).astype(jnp.int32))

    def window(take, t, fill):
        block = jnp.concatenate([take(places[0, t] + i) for i in range(reach)], axis=1)
        block = pltpu.roll(block, places[1, t], 1)[:, :capacity]
        lane = lax.broadcasted_iota(jnp.int32, block.shape, 1)
        return jnp.where(lane < places[2, t], block, fill)

    def code_tile(i):
        return jnp.concatenate([codes_ref[g, i] for g in range(codes_ref.shape[0])], axis=0)

    def pack_codes(t, ref):
        block = window(code_tile, t, OUTSIDE).astype(jnp.float32).astype(jnp.bfloat16)
        for u in range(units):
            ref[t, u] = block[u * UNIT : (u + 1) * UNIT]

    def packed_grads(k, t):
        return window(lambda i: lines_ref[k, i], t, 0.0).astype(jnp.bfloat16)

    def unfold(k):
        for i in range(tiles):
            lines_ref[k, i] = panel_ref[k, :, i * LANES : (i + 1) * LANES].astype(jnp.float32)

    def release(dz, c):
        for k in range(2):
            code_copy(c, ahead(dz, k), row).start()

    codes_load.wait()
    loop(2, 4, lambda i: pack_codes(ahead(1, i - 2), codes_sent))
    loop(0, chunks, lambda c: release(1, c))

    pack_codes(twin, codes_sent)
    loop(0, chunks, lambda c: code_copy(c, twin, row).start())
    pack_codes(row, codes_in)
    loop(4, owners, lambda i: pack_codes(ahead(i // 2, lax.rem(i, 2)), codes_sent))

    own_piece.wait()
    arrive(home(0, groups - 1), group_recv)
    unfold(feat)

    def send_grads(t):
        grads_sent[t] = packed_grads(feat, t)
        grad_copy(t, row).start()

    loop(2, 4, lambda i: send_grads(ahead(1, i - 2)))
    others(unfold)
    for k in range(groups):
        twin_sent[k] = packed_grads(k, twin)
    twin_copy().start()
    for k in range(groups):
        grads_in[row, k] = packed_grads(k, row)
    loop(4, owners, lambda i: send_grads(ahead(i // 2, lax.rem(i, 2))))

    def forward(p):
        grad_copy(row, p).wait_recv()
        others(lambda f: spread_copy(p, f).start())

    def prepare(panels):
        lines = [
            jnp.concatenate([grads_in[p, f].astype(jnp.float32) for f in range(groups)], axis=0)
            for p in panels
        ]
        top = functools.reduce(jnp.maximum, [jnp.max(jnp.abs(v), axis=1, keepdims=True) for v in lines])
        level = jnp.floor(jnp.log2(jnp.maximum(top, 2.0**-110)))
        up, down = jnp.exp2(6.0 - level), jnp.exp2(level - 6.0)
        for h, v in enumerate(lines):
            at = pl.ds(h * capacity, capacity)
            v = v * jnp.broadcast_to(up, v.shape)
            high = v.astype(F8)
            wide_ref[:outputs, at] = high
            wide_ref[outputs:, at] = ((v - high.astype(jnp.float32)) * LOW).astype(F8)
        scale_ref[...] = jnp.broadcast_to(down, scale_ref.shape)

    def multiply(panels, c, add):
        blocks = [[codes_in[p, c * part + u] for u in range(part)] for p in panels]
        tile = product(wide_ref[...], scale_ref[:, :1], blocks)
        size = part * UNIT * BINS
        at = pl.ds(pl.multiple_of(c * size, size), size)
        out_ref[:, at] = out_ref[:, at] + tile if add else tile

    if chips > 1:
        for c in range(2):
            forward(behind(1, c))
    twin_copy().wait_recv()
    prepare((row, twin))

    def first(c):
        if chips > 2:
            release(2, c)
        code_copy(c, row, twin).wait_recv()
        multiply((row, twin), c, False)

    loop(0, 1, first)
    if chips > 2:
        for c in range(2):
            forward(behind(2, c))
    loop(1, chunks, first)

    def phase(dz):
        panels = [behind(dz, c) for c in range(2)]

        @pl.when(jnp.int32(dz + 2) < chips)
        def _():
            for c in range(2):
                forward(behind(dz + 2, c))

        for p in panels:
            arrive(grads_in.at[p, pl.ds(0, groups - 1)], spread_recv.at[p])
        prepare(panels)

        def chunk(c):
            @pl.when(jnp.int32(dz + 2) < chips)
            def _():
                release(dz + 2, c)

            for p in panels:
                code_copy(c, row, p).wait_recv()
            multiply(panels, c, True)

        lax.fori_loop(0, chunks, lambda i, _: (chunk(i), 0)[1], 0)

    lax.fori_loop(1, chips - 1, lambda i, _: (phase(i), 0)[1], 0)

    panels = [behind(chips - 1, c) for c in range(2)]
    for p in panels:
        arrive(grads_in.at[p, pl.ds(0, groups - 1)], spread_recv.at[p])
    prepare(panels)
    for h, p in enumerate(panels):
        for c in range(chunks):
            code_copy(c, row, p).wait_recv()
        last_codes[h] = codes_in[p]

    arrive(home(0, groups - 1), group_send)
    twin_copy().wait_send()
    arrive(codes_sent.at[pl.ds(0, owners - 1)], code_send)
    arrive(grads_sent.at[pl.ds(0, owners - 2)], grad_send)
    arrive(grads_in.at[pl.ds(0, owners - 2), pl.ds(0, groups - 1)], spread_send)


def last_kernel(sums_ref, codes_ref, wide_ref, scale_ref, out_ref, tile_ref, sems):
    chunks, _, size = tile_ref.shape
    part = codes_ref.shape[1] // chunks

    def copy(c):
        return pltpu.make_async_copy(tile_ref.at[c], out_ref.at[:, pl.ds(c * size, size)], sems.at[c])

    for c in range(chunks):
        blocks = [[codes_ref[h, c * part + u] for u in range(part)] for h in range(2)]
        tile = product(wide_ref[...], scale_ref[:, :1], blocks)
        tile_ref[c] = sums_ref[:, pl.ds(c * size, size)] + tile
        copy(c).start()
    for c in range(chunks):
        copy(c).wait()


def last_pair(sums, codes, wide, scale):
    outputs, columns = sums.shape
    chunks = min(codes.shape[1], 2)
    vectors = pl.BlockSpec(memory_space=pltpu.VMEM)
    return pl.pallas_call(
        last_kernel,
        out_shape=jax.ShapeDtypeStruct(sums.shape, jnp.float32),
        in_specs=[vectors] * 4,
        out_specs=pl.BlockSpec(memory_space=pltpu.HBM),
        scratch_shapes=[
            pltpu.VMEM((chunks, outputs, columns // chunks), jnp.float32),
            pltpu.SemaphoreType.DMA((chunks,)),
        ],
        compiler_params=pltpu.CompilerParams(vmem_limit_bytes=16 << 20),
        name="last_pair",
    )(sums, codes, wide, scale)


def on_device(grads, codes, node_ids, node_slot):
    owners = node_slot.shape[0]
    groups = lax.axis_size("feat")
    features, length = codes.shape
    outputs, piece = grads.shape
    share = outputs // groups
    capacity = 2 * length // owners
    tiles = length // LANES
    units = features // UNIT
    chunks = min(units, 2)
    vectors = pl.BlockSpec(memory_space=pltpu.VMEM)
    far = pl.BlockSpec(memory_space=pltpu.HBM)
    dma = pltpu.SemaphoreType.DMA
    parts = pl.pallas_call(
        functools.partial(kernel, chunks=chunks),
        out_shape=(
            jax.ShapeDtypeStruct((outputs, features * BINS), jnp.float32),
            jax.ShapeDtypeStruct((2, units, UNIT, capacity), jnp.bfloat16),
            jax.ShapeDtypeStruct((2 * outputs, 2 * capacity), F8),
            jax.ShapeDtypeStruct((outputs, LANES), jnp.float32),
        ),
        in_specs=[far] * 4,
        out_specs=(vectors,) * 4,
        scratch_shapes=[
            pltpu.SMEM(node_slot.shape, jnp.int32),
            pltpu.SMEM((3, owners), jnp.int32),
            pltpu.VMEM((tiles, LANES), jnp.int32),
            pltpu.VMEM((features // 8, tiles, 8, LANES), jnp.int32),
            pltpu.VMEM((groups, share, length), jnp.bfloat16),
            pltpu.VMEM((groups, tiles, share, LANES), jnp.float32),
            pltpu.VMEM((owners, units, UNIT, capacity), jnp.bfloat16),
            pltpu.VMEM((owners, units, UNIT, capacity), jnp.bfloat16),
            pltpu.VMEM((owners, share, capacity), jnp.bfloat16),
            pltpu.VMEM((owners, groups, share, capacity), jnp.bfloat16),
            pltpu.VMEM((groups, share, capacity), jnp.bfloat16),
            dma,
            dma,
            dma,
            dma,
            dma,
            dma,
            dma,
            dma,
            dma,
            dma((owners, chunks)),
            dma,
            dma((owners,)),
            dma,
            dma((owners,)),
        ],
        compiler_params=pltpu.CompilerParams(
            collective_id=0, has_side_effects=True, vmem_limit_bytes=40 << 20
        ),
        name="exchange_and_multiply",
    )(*[
        pltpu.with_memory_space_constraint(x, pltpu.HBM)
        for x in (
            node_slot, node_ids.reshape(tiles, LANES),
            codes.reshape(features // 8, 8, tiles, LANES).transpose(0, 2, 1, 3),
            grads.reshape(groups, share, piece),
        )
    ])
    return last_pair(*parts)[None]


def solution(mesh):
    in_specs = (P(None, ("row", "feat")), P("feat", "row"), P("row"), P())
    out_specs = P("row", None, "feat")
    return jax.shard_map(
        on_device, mesh=mesh, in_specs=in_specs, out_specs=out_specs, check_vma=False
    )
```

```python
import functools

import jax
import jax.numpy as jnp
from jax import lax
from jax.experimental import pallas as pl
from jax.experimental.pallas import tpu as pltpu
from jax.sharding import PartitionSpec as P

BINS = 128
LANES = 128
OUTSIDE = 255
UNIT = 16
LOW = 32.0
MESH = pl.DeviceIdType.MESH
F8 = jnp.float8_e4m3fn


def loop(start, stop, body):
    if stop - start <= 8:
        for i in range(start, stop):
            body(i)
    else:
        lax.fori_loop(start, stop, lambda i, _: (body(i), 0)[1], 0)


def table_of(line):
    shape = (32, line.shape[1])
    rows = (jnp.broadcast_to(line, shape) - lax.broadcasted_iota(jnp.int32, shape, 0)).astype(jnp.int8)
    one, zero = jnp.ones(shape, F8), jnp.zeros(shape, F8)
    return [jnp.where(rows == jnp.int8(b), one, zero) for b in range(0, BINS, 32)]


def product(wide, scale, blocks):
    def table(units):
        block = [u.astype(jnp.float32).astype(jnp.int32) for u in units]
        return jnp.concatenate([t for b in block for q in range(UNIT) for t in table_of(b[q : q + 1])], axis=0)

    both = lax.dot_general(
        wide, jnp.concatenate([table(units) for units in blocks], axis=1),
        (((1,), (1,)), ((), ())), preferred_element_type=jnp.float32)
    outputs = both.shape[0] // 2
    tile = both[:outputs] + both[outputs:] * (1.0 / LOW)
    return tile * jnp.broadcast_to(scale, tile.shape)


def kernel(
    slots_hbm, ids_hbm, codes_hbm, grads_hbm, out_ref, last_codes, wide_ref, scale_ref,
    slots, places, ids_ref, codes_ref, panel_ref, lines_ref,
    codes_sent, codes_in, grads_sent, grads_in, twin_sent,
    slots_sem, ids_sem, codes_sem, own_sem, twin_send, twin_recv, group_send, group_recv,
    code_send, code_recv, grad_send, grad_recv, spread_send, spread_recv, *, chunks,
):
    owners, units, _, capacity = codes_in.shape
    groups, share, piece = grads_hbm.shape
    tiles = ids_ref.shape[0]
    outputs = groups * share
    chips = owners // 2
    part = units // chunks
    span = capacity + LANES
    reach = span // LANES
    row, feat = lax.axis_index("row"), lax.axis_index("feat")
    chip, core = row // 2, lax.rem(row, 2)
    twin = chip * 2 + 1 - core

    def others(body):
        loop(1, groups, lambda d: body(lax.rem(feat + d, groups)))

    def ahead(dz, c):
        return lax.rem(chip + dz, chips) * 2 + lax.rem(core + c, 2)

    def behind(dz, c):
        return lax.rem(chip + chips - dz, chips) * 2 + lax.rem(core + c, 2)

    def remote(body):
        loop(2, owners, lambda i: body(ahead(i // 2, lax.rem(i, 2))))

    def home(f, pieces=1):
        return panel_ref.at[:, :, pl.ds(pl.multiple_of(f * piece, LANES), pieces * piece)]

    def group_copy(peer):
        return pltpu.make_async_remote_copy(
            grads_hbm, home(feat), group_send, group_recv, (row, peer), MESH
        )

    def twin_copy():
        return pltpu.make_async_remote_copy(
            twin_sent, grads_in.at[row], twin_send, twin_recv, (twin, feat), MESH
        )

    def code_copy(c, peer, owner):
        at = pl.ds(c * part, part)
        return pltpu.make_async_remote_copy(
            codes_sent.at[peer, at], codes_in.at[owner, at],
            code_send, code_recv.at[owner, c], (peer, feat), MESH,
        )

    def grad_copy(peer, owner):
        return pltpu.make_async_remote_copy(
            grads_sent.at[peer], grads_in.at[owner, feat],
            grad_send, grad_recv.at[owner], (peer, feat), MESH,
        )

    def spread_copy(p, peer):
        return pltpu.make_async_remote_copy(
            grads_in.at[p, feat], grads_in.at[p, feat],
            spread_send, spread_recv.at[p], (row, peer), MESH,
        )

    def arrive(ref, sem):
        pltpu.make_async_copy(ref, ref, sem).wait()

    barrier = pltpu.get_barrier_semaphore()
    others(lambda f: pl.semaphore_signal(barrier, 1, device_id=(row, f), device_id_type=MESH))
    loop(1, owners, lambda d: pl.semaphore_signal(
        barrier, 1, device_id=(lax.rem(row + d, owners), feat), device_id_type=MESH))
    slots_load = pltpu.make_async_copy(slots_hbm, slots, slots_sem)
    ids_load = pltpu.make_async_copy(ids_hbm, ids_ref, ids_sem)
    codes_load = pltpu.make_async_copy(codes_hbm, codes_ref, codes_sem)

    own_piece = pltpu.make_async_copy(grads_hbm, home(feat), own_sem)
    slots_load.start()
    ids_load.start()
    codes_load.start()
    pl.semaphore_wait(barrier, owners + groups - 2)
    others(lambda f: group_copy(f).start())
    own_piece.start()

    slots_load.wait()
    ids_load.wait()
    ids = ids_ref[...]
    for t in range(owners):
        first = jnp.sum((ids < slots[t]).astype(jnp.int32))
        tile = jnp.minimum(first // LANES, tiles - reach)
        places[0, t] = tile
        places[1, t] = lax.rem(span - (first - tile * LANES), span)
        places[2, t] = jnp.sum((ids == slots[t]).astype(jnp.int32))

    def window(take, t, fill):
        block = jnp.concatenate([take(places[0, t] + i) for i in range(reach)], axis=1)
        block = pltpu.roll(block, places[1, t], 1)[:, :capacity]
        lane = lax.broadcasted_iota(jnp.int32, block.shape, 1)
        return jnp.where(lane < places[2, t], block, fill)

    def code_tile(i):
        return jnp.concatenate([codes_ref[g, i] for g in range(codes_ref.shape[0])], axis=0)

    def pack_codes(t, ref):
        block = window(code_tile, t, OUTSIDE).astype(jnp.float32).astype(jnp.bfloat16)
        for u in range(units):
            ref[t, u] = block[u * UNIT : (u + 1) * UNIT]

    def packed_grads(k, t):
        return window(lambda i: lines_ref[k, i], t, 0.0).astype(jnp.bfloat16)

    def unfold(k):
        for i in range(tiles):
            lines_ref[k, i] = panel_ref[k, :, i * LANES : (i + 1) * LANES].astype(jnp.float32)

    def release(dz, c):
        for k in range(2):
            code_copy(c, ahead(dz, k), row).start()

    codes_load.wait()
    loop(2, 4, lambda i: pack_codes(ahead(1, i - 2), codes_sent))
    loop(0, chunks, lambda c: release(1, c))

    pack_codes(twin, codes_sent)
    loop(0, chunks, lambda c: code_copy(c, twin, row).start())
    pack_codes(row, codes_in)
    loop(4, owners, lambda i: pack_codes(ahead(i // 2, lax.rem(i, 2)), codes_sent))

    own_piece.wait()
    arrive(home(0, groups - 1), group_recv)
    unfold(feat)

    def send_grads(t):
        grads_sent[t] = packed_grads(feat, t)
        grad_copy(t, row).start()

    loop(2, 4, lambda i: send_grads(ahead(1, i - 2)))
    others(unfold)
    for k in range(groups):
        twin_sent[k] = packed_grads(k, twin)
    twin_copy().start()
    for k in range(groups):
        grads_in[row, k] = packed_grads(k, row)
    loop(4, owners, lambda i: send_grads(ahead(i // 2, lax.rem(i, 2))))

    def forward(p):
        grad_copy(row, p).wait_recv()
        others(lambda f: spread_copy(p, f).start())

    def prepare(panels):
        lines = [
            jnp.concatenate([grads_in[p, f].astype(jnp.float32) for f in range(groups)], axis=0)
            for p in panels
        ]
        top = functools.reduce(jnp.maximum, [jnp.max(jnp.abs(v), axis=1, keepdims=True) for v in lines])
        level = jnp.floor(jnp.log2(jnp.maximum(top, 2.0**-110)))
        up, down = jnp.exp2(6.0 - level), jnp.exp2(level - 6.0)
        for h, v in enumerate(lines):
            at = pl.ds(h * capacity, capacity)
            v = v * jnp.broadcast_to(up, v.shape)
            high = v.astype(F8)
            wide_ref[:outputs, at] = high
            wide_ref[outputs:, at] = ((v - high.astype(jnp.float32)) * LOW).astype(F8)
        scale_ref[...] = jnp.broadcast_to(down, scale_ref.shape)

    def multiply(panels, c, add):
        blocks = [[codes_in[p, c * part + u] for u in range(part)] for p in panels]
        tile = product(wide_ref[...], scale_ref[:, :1], blocks)
        size = part * UNIT * BINS
        at = pl.ds(pl.multiple_of(c * size, size), size)
        out_ref[:, at] = out_ref[:, at] + tile if add else tile

    if chips > 1:
        for c in range(2):
            forward(behind(1, c))
    twin_copy().wait_recv()
    prepare((row, twin))

    def first(c):
        if chips > 2:
            release(2, c)
        code_copy(c, row, twin).wait_recv()
        multiply((row, twin), c, False)

    loop(0, 1, first)
    if chips > 2:
        for c in range(2):
            forward(behind(2, c))
    loop(1, chunks, first)

    def phase(dz):
        panels = [behind(dz, c) for c in range(2)]

        @pl.when(jnp.int32(dz + 2) < chips)
        def _():
            for c in range(2):
                forward(behind(dz + 2, c))

        for p in panels:
            arrive(grads_in.at[p, pl.ds(0, groups - 1)], spread_recv.at[p])
        prepare(panels)

        def chunk(c):
            @pl.when(jnp.int32(dz + 2) < chips)
            def _():
                release(dz + 2, c)

            for p in panels:
                code_copy(c, row, p).wait_recv()
            multiply(panels, c, True)

        lax.fori_loop(0, chunks, lambda i, _: (chunk(i), 0)[1], 0)

    lax.fori_loop(1, chips - 1, lambda i, _: (phase(i), 0)[1], 0)

    panels = [behind(chips - 1, c) for c in range(2)]
    for p in panels:
        arrive(grads_in.at[p, pl.ds(0, groups - 1)], spread_recv.at[p])
    prepare(panels)
    for h, p in enumerate(panels):
        for c in range(chunks):
            code_copy(c, row, p).wait_recv()
        last_codes[h] = codes_in[p]

    arrive(home(0, groups - 1), group_send)
    twin_copy().wait_send()
    arrive(codes_sent.at[pl.ds(0, owners - 1)], code_send)
    arrive(grads_sent.at[pl.ds(0, owners - 2)], grad_send)
    arrive(grads_in.at[pl.ds(0, owners - 2), pl.ds(0, groups - 1)], spread_send)


def last_kernel(sums_ref, codes_ref, wide_ref, scale_ref, out_ref, tile_ref, sems):
    units = codes_ref.shape[1]
    size = UNIT * BINS
    cuts = sorted({0, units // 2, units - units // 4, units})
    copies = []
    for c, (low, high) in enumerate(zip(cuts[:-1], cuts[1:])):
        at = pl.ds(low * size, (high - low) * size)
        blocks = [[codes_ref[h, u] for u in range(low, high)] for h in range(2)]
        tile_ref[:, at] = sums_ref[:, at] + product(wide_ref[...], scale_ref[:, :1], blocks)
        copies.append(pltpu.make_async_copy(tile_ref.at[:, at], out_ref.at[:, at], sems.at[c]))
        copies[-1].start()
    for copy in copies:
        copy.wait()


def last_pair(sums, codes, wide, scale):
    vectors = pl.BlockSpec(memory_space=pltpu.VMEM)
    return pl.pallas_call(
        last_kernel,
        out_shape=jax.ShapeDtypeStruct(sums.shape, jnp.float32),
        in_specs=[vectors] * 4,
        out_specs=pl.BlockSpec(memory_space=pltpu.HBM),
        scratch_shapes=[
            pltpu.VMEM(sums.shape, jnp.float32),
            pltpu.SemaphoreType.DMA((3,)),
        ],
        compiler_params=pltpu.CompilerParams(vmem_limit_bytes=16 << 20),
        name="last_pair",
    )(sums, codes, wide, scale)


def on_device(grads, codes, node_ids, node_slot):
    owners = node_slot.shape[0]
    groups = lax.axis_size("feat")
    features, length = codes.shape
    outputs, piece = grads.shape
    share = outputs // groups
    capacity = 2 * length // owners
    tiles = length // LANES
    units = features // UNIT
    chunks = min(units, 2)
    vectors = pl.BlockSpec(memory_space=pltpu.VMEM)
    far = pl.BlockSpec(memory_space=pltpu.HBM)
    dma = pltpu.SemaphoreType.DMA
    parts = pl.pallas_call(
        functools.partial(kernel, chunks=chunks),
        out_shape=(
            jax.ShapeDtypeStruct((outputs, features * BINS), jnp.float32),
            jax.ShapeDtypeStruct((2, units, UNIT, capacity), jnp.bfloat16),
            jax.ShapeDtypeStruct((2 * outputs, 2 * capacity), F8),
            jax.ShapeDtypeStruct((outputs, LANES), jnp.float32),
        ),
        in_specs=[far] * 4,
        out_specs=(vectors,) * 4,
        scratch_shapes=[
            pltpu.SMEM(node_slot.shape, jnp.int32),
            pltpu.SMEM((3, owners), jnp.int32),
            pltpu.VMEM((tiles, LANES), jnp.int32),
            pltpu.VMEM((features // 8, tiles, 8, LANES), jnp.int32),
            pltpu.VMEM((groups, share, length), jnp.bfloat16),
            pltpu.VMEM((groups, tiles, share, LANES), jnp.float32),
            pltpu.VMEM((owners, units, UNIT, capacity), jnp.bfloat16),
            pltpu.VMEM((owners, units, UNIT, capacity), jnp.bfloat16),
            pltpu.VMEM((owners, share, capacity), jnp.bfloat16),
            pltpu.VMEM((owners, groups, share, capacity), jnp.bfloat16),
            pltpu.VMEM((groups, share, capacity), jnp.bfloat16),
            dma,
            dma,
            dma,
            dma,
            dma,
            dma,
            dma,
            dma,
            dma,
            dma((owners, chunks)),
            dma,
            dma((owners,)),
            dma,
            dma((owners,)),
        ],
        compiler_params=pltpu.CompilerParams(
            collective_id=0, has_side_effects=True, vmem_limit_bytes=40 << 20
        ),
        name="exchange_and_multiply",
    )(*[
        pltpu.with_memory_space_constraint(x, pltpu.HBM)
        for x in (
            node_slot, node_ids.reshape(tiles, LANES),
            codes.reshape(features // 8, 8, tiles, LANES).transpose(0, 2, 1, 3),
            grads.reshape(groups, share, piece),
        )
    ])
    return last_pair(*parts)[None]


def solution(mesh):
    in_specs = (P(None, ("row", "feat")), P("feat", "row"), P("row"), P())
    out_specs = P("row", None, "feat")
    return jax.shard_map(
        on_device, mesh=mesh, in_specs=in_specs, out_specs=out_specs, check_vma=False
    )
```
